128 devices in a mesh: occ: 8 (over y_hi, z), virt: 16 (over x, y_lo, core).
Axes of the slice: x: 4, y: 4 (y_hi: 2, y_lo: 2; y = y_hi * 2 + y_lo), z: 4, core: 2. Of those that a mesh axis runs over, the one named last changes fastest.
Arguments:
- basis_integrals: bfloat16 [32, 1280, 2048], P(None, 'virt', 'occ'), may hold values from -2 to 2
- group_sizes: int32 [8], replicated, may hold values from 1 to 6, 32 in all
- orbital_order: int32 [32], replicated, may hold values from 0 to 31, each once
- eps_occ: float32 [32], replicated, may hold values from -1.5 to -0.3
- eps_vir: float32 [1280], replicated, may hold values from 0.2 to 2.5
Outputs:
- density: bfloat16 [8, 6, 1280, 2048], P('occ', None, 'virt')
The draws below stay inside these ranges and needn't reach their ends.
Inputs may be any that keep to these rules, and one draw needn't show every extreme that they name: `group_sizes`: each group holds 1 to 6 orbitals, 32 together, and some group holds exactly 6. `orbital_order`: each window orbital appears once.
All inputs are finite; a program needn't handle non-finite values.
Results may differ from the reference program's by a relative error of at most 0.0034.
Values may be sent and summed in bfloat16 or wider, within the bound.
A program may use at most 64 MiB of HBM per device.

```python
import math
import jax
import jax.numpy as jnp
import numpy as np
from jax import lax

NVIR = 1280
NAUX = 2048
CAP = 6
NW = 32
N_OCC = 8


def block_scale(rng, extent, split, low, high):
    loudness, own = 1.0, jax.random.fold_in(rng, 6)
    for dim, parts in split:
        steps = jnp.exp(jax.random.uniform(jax.random.fold_in(own, dim), (parts,), jnp.float32, low / len(split), high / len(split)))
        loudness = loudness * jnp.repeat(steps, extent[dim] // parts).reshape([-1 if axis == dim else 1 for axis in range(len(extent))])
    return loudness


def profile(number_of, total, bound, slope):
    loads = [(1 << 20) // math.isqrt(grade ** slope) + 1 for grade in range(2, number_of + 1)]
    surplus, counts = total - bound - (number_of - 1), [1] * (number_of - 1)
    while surplus > 0:
        free = [i for i in range(number_of - 1) if counts[i] < bound]
        pool, remaining = sum([loads[i] for i in free]), surplus
        for i in free:
            extra = min(bound - counts[i], max(1, remaining * loads[i] // pool), surplus)
            counts[i] = counts[i] + extra
            surplus = surplus - extra
    return np.array([bound] + counts)


def uneven_parts(own_key, amount, total, reach, skew):
    if amount == 2:
        one = jax.random.randint(own_key, (), max(1, total - reach), min(reach, total - 1) + 1)
        return jnp.stack([one, total - one])
    lengths = jnp.asarray(profile(amount, total, reach, skew), jnp.int32)
    pairs = (amount - 1) // 2
    donor, receiver = lengths[1:1 + 2 * pairs:2], lengths[2:2 + 2 * pairs:2]
    room = jnp.minimum(donor - 1, reach - receiver)
    passed = jax.random.randint(jax.random.fold_in(own_key, 1), (pairs,), 0, 1 << 20) % (room + 1)
    lengths = lengths.at[1:1 + 2 * pairs:2].set(donor - passed).at[2:2 + 2 * pairs:2].set(receiver + passed)
    return lengths[jax.random.permutation(jax.random.fold_in(own_key, 2), amount)]


def scatter_about(own_key, extent, deviation, limit, cuts=(), kind=jnp.bfloat16):
    drawn = deviation * jax.random.normal(own_key, extent, jnp.float32)
    if cuts:
        drawn = drawn * block_scale(own_key, extent, cuts, -0.22, 0.18)
    return jnp.clip(drawn, -limit, limit).astype(kind)


def setup_inputs(seed: int = 0) -> dict:
    key_of = jax.random.split(jax.random.key(seed), 6)
    basis_integrals = scatter_about(key_of[0], (NW, NVIR, NAUX), (NAUX ** -0.25), 2.0, ((1, 16), (2, 8)))
    group_sizes = uneven_parts(key_of[1], N_OCC, NW, CAP, 1).astype(jnp.int32)
    orbital_order = jax.random.permutation(key_of[2], NW).astype(jnp.int32)
    eps_occ = jnp.clip(jax.random.uniform(key_of[3], (NW,), jnp.float32, -1.5, -0.3), -1.5, -0.3)
    eps_vir = jnp.clip(jax.random.uniform(key_of[4], (NVIR,), jnp.float32, 0.2, 2.5), 0.2, 2.5)
    return dict(basis_integrals=basis_integrals, group_sizes=group_sizes, orbital_order=orbital_order, eps_occ=eps_occ, eps_vir=eps_vir)


def reference(basis_integrals, group_sizes, orbital_order, eps_occ, eps_vir):
    slot_index = jnp.arange(CAP, dtype=jnp.int32)
    offsets = (jnp.cumsum(group_sizes) - group_sizes).astype(jnp.int32)
    occupied = slot_index[None, :] < group_sizes[:, None]
    position = jnp.clip(offsets[:, None] + slot_index[None, :], 0, NW - 1).astype(jnp.int32)
    orbital = jnp.where(occupied, orbital_order[position], 0).astype(jnp.int32)

    def one_group(group_args):
        orbitals, alive = group_args
        slot_mask = jnp.where(alive, 1.0, 0.0).astype(jnp.bfloat16)
        selected = basis_integrals[orbitals] * slot_mask[:, None, None]
        flattened = selected.reshape(CAP * NVIR, NAUX).astype(jnp.float32)
        coulomb = jnp.dot(flattened, flattened.T, precision=lax.Precision.HIGHEST)
        occ_energy = jnp.where(alive, eps_occ[orbitals], jnp.float32(0.0))
        row_gap = (occ_energy[:, None] - eps_vir[None, :]).reshape(-1)
        amplitude = coulomb / (row_gap[:, None] + row_gap[None, :])
        amp_four = amplitude.reshape(CAP, NVIR, CAP, NVIR)
        combined = (2.0 * amp_four - amp_four.transpose(2, 1, 0, 3)).reshape(CAP * NVIR, CAP * NVIR)
        combined = combined.astype(jnp.bfloat16).astype(jnp.float32)
        density = jnp.dot(combined, flattened, precision=lax.Precision.HIGHEST)
        return density.reshape(CAP, NVIR, NAUX).astype(jnp.bfloat16)

    return lax.map(one_group, (orbital, occupied))
```

```python
import functools

import jax
import jax.numpy as jnp
from jax import lax
from jax.experimental import pallas as pl
from jax.experimental.pallas import tpu as pltpu
from jax.sharding import PartitionSpec as P

CAP = 6
N_OCC = 8
N_VIRT = 16
ROWS = 16
MESH = pl.DeviceIdType.MESH

LEFT, RIGHT, ACROSS, FAR_A, FAR_B, LEFT_X, RIGHT_X, FAR_X = range(8)
N_LINK = 8
B_OWN, B_LEFT, B_RIGHT, B_ACROSS, B_FAR, B_LEFT_X, B_RIGHT_X, B_FAR_X = range(8)
N_SIB = 8


def kernel(
    phases, outgoing, row_gap, col_gap, out, whole, own, coul, amp, acc,
    a2a_send, a2a_recv, link_send, link_recv, sib_send, sib_recv, local_sem,
):
    occ = lax.axis_index("occ")
    me = lax.axis_index("virt")
    x, y, core = me // 4, (me // 2) % 2, me % 2
    slab = outgoing.shape[3]
    width = N_VIRT * ROWS

    def block(dx, flip):
        return ((x + dx) % 4) * 4 + (y + flip) % 2 * 2 + core

    right, left, across = block(1, 0), block(3, 0), block(0, 1)
    sibling = me + 1 - 2 * core

    barrier = pltpu.get_barrier_semaphore()
    for d in range(1, N_OCC):
        pl.semaphore_signal(
            barrier, inc=1, device_id={"occ": (occ + d) % N_OCC}, device_id_type=MESH
        )
    for peer in (right, left, across, sibling):
        pl.semaphore_signal(barrier, inc=1, device_id={"virt": peer}, device_id_type=MESH)
    pl.semaphore_wait(barrier, N_OCC + 3)

    my_slab = pl.ds(pl.multiple_of(occ * slab, slab), slab)

    def exchange(q, d):
        target = (occ + d) % N_OCC
        rows = pl.ds(pl.multiple_of(q * ROWS, ROWS), ROWS)
        return pltpu.make_async_remote_copy(
            src_ref=outgoing.at[target, :, rows, :],
            dst_ref=whole.at[q, :, me, :, my_slab],
            send_sem=a2a_send.at[q, d - 1],
            recv_sem=a2a_recv.at[q, d - 1],
            device_id={"occ": target},
            device_id_type=MESH,
        )

    def keep(q):
        rows = pl.ds(pl.multiple_of(q * ROWS, ROWS), ROWS)
        return pltpu.make_async_copy(
            outgoing.at[occ, :, rows, :], whole.at[q, :, me, :, my_slab], local_sem.at[q]
        )

    def link(q, source, kind, peer, first=0, count=CAP):
        part = whole.at[q, pl.ds(first, count), source]
        return pltpu.make_async_remote_copy(
            src_ref=part, dst_ref=part,
            send_sem=link_send.at[q, kind], recv_sem=link_recv.at[q, kind],
            device_id={"virt": peer}, device_id_type=MESH,
        )

    half = CAP // 2
    sends = {
        LEFT: (lambda q: link(q, me, LEFT, right)),
        RIGHT: (lambda q: link(q, me, RIGHT, left)),
        ACROSS: (lambda q: link(q, me, ACROSS, across)),
        FAR_A: (lambda q: link(q, left, FAR_A, right, 0, half)),
        FAR_B: (lambda q: link(q, right, FAR_B, left, half, CAP - half)),
        LEFT_X: (lambda q: link(q, across, LEFT_X, right)),
        RIGHT_X: (lambda q: link(q, across, RIGHT_X, left)),
        FAR_X: (lambda q: link(q, block(2, 0), FAR_X, across)),
    }
    held = {
        B_OWN: me, B_LEFT: left, B_RIGHT: right, B_ACROSS: across, B_FAR: block(2, 0),
        B_LEFT_X: block(3, 1), B_RIGHT_X: block(1, 1), B_FAR_X: block(2, 1),
    }

    def share(q, kind):
        part = whole.at[q, :, held[kind]]
        return pltpu.make_async_remote_copy(
            src_ref=part, dst_ref=part,
            send_sem=sib_send.at[q, kind], recv_sem=sib_recv.at[q, kind],
            device_id={"virt": sibling}, device_id_type=MESH,
        )

    def launch(q, _):
        for d in range(1, N_OCC):
            exchange(q, d).start()
        keep(q).start()
        return 0

    lax.fori_loop(0, phases, launch, 0)
    acc[...] = jnp.zeros_like(acc)

    def begin(q):
        for d in range(1, N_OCC):
            exchange(q, d).wait_recv()
        keep(q).wait()
        for kind in (LEFT, RIGHT, ACROSS):
            sends[kind](q).start()
        share(q, B_OWN).start()
        own[pl.ds(pl.multiple_of(q * CAP * ROWS, ROWS), CAP * ROWS), :] = whole[q, :, me].reshape(
            CAP * ROWS, own.shape[1]
        )

    def forward(q):
        sends[LEFT](q).wait_recv()
        sends[FAR_A](q).start()
        share(q, B_LEFT).start()
        sends[RIGHT](q).wait_recv()
        sends[FAR_B](q).start()
        share(q, B_RIGHT).start()
        sends[ACROSS](q).wait_recv()
        sends[LEFT_X](q).start()
        sends[RIGHT_X](q).start()
        share(q, B_ACROSS).start()

    def relay(q):
        sends[FAR_A](q).wait_recv()
        sends[FAR_B](q).wait_recv()
        sends[FAR_X](q).start()
        share(q, B_FAR).start()
        sends[LEFT_X](q).wait_recv()
        share(q, B_LEFT_X).start()
        sends[RIGHT_X](q).wait_recv()
        share(q, B_RIGHT_X).start()

    def last(q):
        sends[FAR_X](q).wait_recv()
        share(q, B_FAR_X).start()

    def compute(q):
        for kind in range(N_SIB):
            share(q, kind).wait_recv()

        def coulomb(j, _):
            coul[j] = lax.dot_general(
                own[...], whole[q, j].reshape(width, own.shape[1]),
                (((1,), (1,)), ((), ())), preferred_element_type=jnp.float32,
            )
            return 0

        lax.fori_loop(0, CAP, coulomb, 0)

        def combine(p, _):
            for i in range(CAP):
                at_i = pl.ds(pl.multiple_of(p * CAP * ROWS + i * ROWS, ROWS), ROWS)
                gap_i = row_gap[at_i, :]
                for j in range(i, CAP):
                    at_j = pl.ds(pl.multiple_of(p * CAP * ROWS + j * ROWS, ROWS), ROWS)
                    inverse = 1.0 / (gap_i + col_gap[q, pl.ds(j, 1), :])
                    direct = coul[j, at_i, :]
                    swapped = coul[i, at_j, :]
                    amp[at_i, j * width:(j + 1) * width] = (
                        (2.0 * direct - swapped) * inverse
                    ).astype(jnp.bfloat16)
                    if i != j:
                        amp[at_j, i * width:(i + 1) * width] = (
                            (2.0 * swapped - direct) * inverse
                        ).astype(jnp.bfloat16)
            return 0

        lax.fori_loop(0, phases, combine, 0)

        def density(n, _):
            at = pl.ds(pl.multiple_of(n * 256, 256), 256)
            acc[:, at] += jnp.dot(
                amp[...], whole[q, :, :, :, at].reshape(CAP * width, 256),
                preferred_element_type=jnp.float32,
            )
            return 0

        lax.fori_loop(0, acc.shape[1] // 256, density, 0)

    def step(t, _):
        pl.when(t < phases)(lambda: begin(t))
        pl.when((t >= 1) & (t < phases + 1))(lambda: forward(t - 1))
        pl.when((t >= 2) & (t < phases + 2))(lambda: relay(t - 2))
        pl.when((t >= 3) & (t < phases + 3))(lambda: last(t - 3))
        pl.when(t >= 4)(lambda: compute(t - 4))
        return 0

    lax.fori_loop(0, phases + 4, step, 0)

    for q in range(phases):
        for i in range(CAP):
            row = (q * CAP + i) * ROWS
            out[i, q * ROWS:(q + 1) * ROWS, :] = acc[row:row + ROWS, :].astype(out.dtype)

    def drain(q, _):
        for d in range(1, N_OCC):
            exchange(q, d).wait_send()
        for kind in range(N_LINK):
            sends[kind](q).wait_send()
        for kind in range(N_SIB):
            share(q, kind).wait_send()
        return 0

    lax.fori_loop(0, phases, drain, 0)


def on_device(basis_integrals, group_sizes, orbital_order, eps_occ, eps_vir):
    me_occ = lax.axis_index("occ")
    me_virt = lax.axis_index("virt")
    window, vir_width, slab = basis_integrals.shape
    phases = vir_width // ROWS
    naux = slab * N_OCC
    slot_index = jnp.arange(CAP, dtype=jnp.int32)
    offsets = jnp.cumsum(group_sizes) - group_sizes
    occupied = slot_index[None, :] < group_sizes[:, None]
    position = jnp.clip(offsets[:, None] + slot_index[None, :], 0, window - 1)
    orbital = jnp.where(occupied, orbital_order[position], 0)
    slot_mask = jnp.where(occupied, 1.0, 0.0).astype(jnp.bfloat16)
    outgoing = basis_integrals[orbital] * slot_mask[:, :, None, None]
    my_orbitals = lax.dynamic_index_in_dim(orbital, me_occ, 0, keepdims=False)
    my_alive = lax.dynamic_index_in_dim(occupied, me_occ, 0, keepdims=False)
    occ_energy = jnp.where(my_alive, eps_occ[my_orbitals], jnp.float32(0.0))
    by_phase = eps_vir.reshape(N_VIRT, phases, ROWS).transpose(1, 0, 2)
    own_energy = lax.dynamic_index_in_dim(by_phase, me_virt, 1, keepdims=False)
    row_gap = (occ_energy[None, :, None] - own_energy[:, None, :]).reshape(-1, 1)
    col_gap = occ_energy[None, :, None] - by_phase.reshape(phases, 1, N_VIRT * ROWS)
    rows, width = phases * CAP * ROWS, N_VIRT * ROWS
    dma = pltpu.SemaphoreType.DMA
    density = pl.pallas_call(
        functools.partial(kernel, phases),
        out_shape=jax.ShapeDtypeStruct((CAP, vir_width, naux), jnp.bfloat16),
        in_specs=[
            pl.BlockSpec(memory_space=pl.ANY),
            pl.BlockSpec(memory_space=pltpu.VMEM),
            pl.BlockSpec(memory_space=pltpu.VMEM),
        ],
        out_specs=pl.BlockSpec(memory_space=pltpu.VMEM),
        scratch_shapes=[
            pltpu.VMEM((phases, CAP, N_VIRT, ROWS, naux), jnp.bfloat16),
            pltpu.VMEM((rows, naux), jnp.bfloat16),
            pltpu.VMEM((CAP, rows, width), jnp.float32),
            pltpu.VMEM((rows, CAP * width), jnp.bfloat16),
            pltpu.VMEM((rows, naux), jnp.float32),
            dma((phases, N_OCC - 1)),
            dma((phases, N_OCC - 1)),
            dma((phases, N_LINK)),
            dma((phases, N_LINK)),
            dma((phases, N_SIB)),
            dma((phases, N_SIB)),
            dma((phases,)),
        ],
        compiler_params=pltpu.CompilerParams(
            collective_id=0, has_side_effects=True, vmem_limit_bytes=60 * 1024 * 1024
        ),
    )(outgoing, row_gap, col_gap)
    return density[None]


def solution(mesh):
    return jax.shard_map(
        on_device,
        mesh=mesh,
        in_specs=(P(None, "virt", "occ"), P(), P(), P(), P()),
        out_specs=P("occ", None, "virt", None),
        check_vma=False,
    )
```

```python
import functools

import jax
import jax.numpy as jnp
from jax import lax
from jax.experimental import pallas as pl
from jax.experimental.pallas import tpu as pltpu
from jax.sharding import PartitionSpec as P

CAP = 6
N_OCC = 8
N_VIRT = 16
ROWS = 16
HALF = 8 * ROWS
MESH = pl.DeviceIdType.MESH

LEFT, RIGHT, ACROSS, FAR_A, FAR_B, LEFT_X, RIGHT_X, FAR_X = range(8)
N_LINK = 8
B_OWN, B_LEFT, B_RIGHT, B_ACROSS, B_FAR, B_LEFT_X, B_RIGHT_X, B_FAR_X = range(8)
N_SIB = 8


def kernel(
    phases, sizes, order, eps_occ, basis, eps_vir, out,
    whole, own, coul, amp, acc, outgoing, row_gap, col_gap,
    a2a_send, a2a_recv, link_send, link_recv, sib_send, sib_recv, local_sem,
):
    occ = lax.axis_index("occ")
    me = lax.axis_index("virt")
    x, y, core = me // 4, (me // 2) % 2, me % 2
    slab = outgoing.shape[4]
    rows_per = CAP * ROWS

    def device(dx, flip):
        return (x + dx) % 4 * 4 + (y + flip) % 2 * 2 + core

    def place(dx, flip):
        return (y + flip) % 2, (x + dx) % 4 * 2 + core

    right, left, across = device(1, 0), device(3, 0), device(0, 1)
    sibling = me + 1 - 2 * core
    column_of = x * 2 + core
    mine = place(0, 0)

    barrier = pltpu.get_barrier_semaphore()
    for d in range(1, N_OCC):
        pl.semaphore_signal(
            barrier, inc=1, device_id={"occ": (occ + d) % N_OCC}, device_id_type=MESH
        )
    for peer in (right, left, across, sibling):
        pl.semaphore_signal(barrier, inc=1, device_id={"virt": peer}, device_id_type=MESH)

    offset = jnp.int32(0)
    energy = [jnp.float32(0.0)] * CAP
    for g in range(N_OCC):
        size = sizes[g]
        for s in range(CAP):
            orbital = order[jnp.minimum(offset + s, order.shape[0] - 1)]
            alive = jnp.where(s < size, 1.0, 0.0)
            block = basis[orbital] * jnp.full((phases * ROWS, slab), alive).astype(jnp.bfloat16)
            for q in range(phases):
                outgoing[q, g, s] = block[q * ROWS:(q + 1) * ROWS]
            energy[s] = jnp.where(occ == g, alive * eps_occ[orbital], energy[s])
        offset = offset + size
    pl.semaphore_wait(barrier, N_OCC + 3)

    my_slab = pl.ds(pl.multiple_of(occ * slab, slab), slab)

    def exchange(q, d):
        target = (occ + d) % N_OCC
        return pltpu.make_async_remote_copy(
            src_ref=outgoing.at[q, target],
            dst_ref=whole.at[q, y, :, column_of, :, my_slab],
            send_sem=a2a_send.at[q, d - 1],
            recv_sem=a2a_recv.at[q, d - 1],
            device_id={"occ": target},
            device_id_type=MESH,
        )

    def keep(q):
        return pltpu.make_async_copy(
            outgoing.at[q, occ], whole.at[q, y, :, column_of, :, my_slab], local_sem.at[q]
        )

    def link(q, source, kind, peer, first=0, count=CAP):
        part = whole.at[q, source[0], pl.ds(first, count), source[1]]
        return pltpu.make_async_remote_copy(
            src_ref=part, dst_ref=part,
            send_sem=link_send.at[q, kind], recv_sem=link_recv.at[q, kind],
            device_id={"virt": peer}, device_id_type=MESH,
        )

    half = CAP // 2
    sends = {
        LEFT: (lambda q: link(q, mine, LEFT, right)),
        RIGHT: (lambda q: link(q, mine, RIGHT, left)),
        ACROSS: (lambda q: link(q, mine, ACROSS, across)),
        FAR_A: (lambda q: link(q, place(3, 0), FAR_A, right, 0, half)),
        FAR_B: (lambda q: link(q, place(1, 0), FAR_B, left, half, CAP - half)),
        LEFT_X: (lambda q: link(q, place(0, 1), LEFT_X, right)),
        RIGHT_X: (lambda q: link(q, place(0, 1), RIGHT_X, left)),
        FAR_X: (lambda q: link(q, place(2, 0), FAR_X, across)),
    }
    held = {
        B_OWN: mine, B_LEFT: place(3, 0), B_RIGHT: place(1, 0), B_ACROSS: place(0, 1),
        B_FAR: place(2, 0), B_LEFT_X: place(3, 1), B_RIGHT_X: place(1, 1), B_FAR_X: place(2, 1),
    }

    def share(q, kind):
        part = whole.at[q, held[kind][0], :, held[kind][1]]
        return pltpu.make_async_remote_copy(
            src_ref=part, dst_ref=part,
            send_sem=sib_send.at[q, kind], recv_sem=sib_recv.at[q, kind],
            device_id={"virt": sibling}, device_id_type=MESH,
        )

    def launch(q, _):
        for d in range(1, N_OCC):
            exchange(q, d).start()
        keep(q).start()
        return 0

    lax.fori_loop(0, phases, launch, 0)

    lane = lax.broadcasted_iota(jnp.int32, (ROWS, HALF), 1)
    sub = lax.broadcasted_iota(jnp.int32, (ROWS, HALF), 0)
    first_lane = column_of * ROWS
    for q in range(phases):
        spread = jnp.broadcast_to(eps_vir[pl.ds(q * 2 + y, 1), :], (ROWS, HALF))
        column = jnp.sum(
            jnp.where(lane == sub + first_lane, spread, 0.0), axis=1, keepdims=True
        )
        for i in range(CAP):
            at = (q * CAP + i) * ROWS
            row_gap[at:at + ROWS, :] = energy[i] - jnp.broadcast_to(column, (ROWS, HALF))
            for h in range(2):
                col_gap[q, h, i:i + 1, :] = energy[i] - eps_vir[q * 2 + h:q * 2 + h + 1, :]
    acc[...] = jnp.zeros_like(acc)

    def begin(q):
        for d in range(1, N_OCC):
            exchange(q, d).wait_recv()
        keep(q).wait()
        for kind in (LEFT, RIGHT, ACROSS):
            sends[kind](q).start()
        share(q, B_OWN).start()
        own[pl.ds(pl.multiple_of(q * rows_per, rows_per), rows_per), :] = whole[q, y, :, column_of].reshape(
            rows_per, own.shape[1]
        )

    def forward(q):
        sends[LEFT](q).wait_recv()
        sends[FAR_A](q).start()
        share(q, B_LEFT).start()
        sends[RIGHT](q).wait_recv()
        sends[FAR_B](q).start()
        share(q, B_RIGHT).start()
        sends[ACROSS](q).wait_recv()
        sends[LEFT_X](q).start()
        sends[RIGHT_X](q).start()
        share(q, B_ACROSS).start()

    def relay_far(q):
        sends[FAR_A](q).wait_recv()
        sends[FAR_B](q).wait_recv()
        sends[FAR_X](q).start()
        share(q, B_FAR).start()

    def relay_rest(q):
        sends[LEFT_X](q).wait_recv()
        share(q, B_LEFT_X).start()
        sends[RIGHT_X](q).wait_recv()
        share(q, B_RIGHT_X).start()
        sends[FAR_X](q).wait_recv()
        share(q, B_FAR_X).start()

    def compute(q, h, kinds):
        for kind in kinds:
            share(q, kind).wait_recv()

        def coulomb(j, _):
            coul[j] = lax.dot_general(
                own[...], whole[q, h, pl.ds(j * 2, 2)].reshape(2 * HALF, own.shape[1]),
                (((1,), (1,)), ((), ())), preferred_element_type=jnp.float32,
            )
            return 0

        lax.fori_loop(0, CAP // 2, coulomb, 0)

        def combine(p, _):
            def lanes(j):
                return slice(j % 2 * HALF, (j % 2 + 1) * HALF)

            for i in range(CAP):
                at_i = pl.ds(pl.multiple_of(p * rows_per + i * ROWS, ROWS), ROWS)
                gap_i = row_gap[at_i, :]
                for j in range(i, CAP):
                    at_j = pl.ds(pl.multiple_of(p * rows_per + j * ROWS, ROWS), ROWS)
                    inverse = 1.0 / (gap_i + col_gap[q, h, pl.ds(j, 1), :])
                    direct = coul[j // 2, at_i, lanes(j)]
                    swapped = coul[i // 2, at_j, lanes(i)]
                    amp[at_i, j * HALF:(j + 1) * HALF] = (
                        (2.0 * direct - swapped) * inverse
                    ).astype(jnp.bfloat16)
                    if i != j:
                        amp[at_j, i * HALF:(i + 1) * HALF] = (
                            (2.0 * swapped - direct) * inverse
                        ).astype(jnp.bfloat16)
            return 0

        lax.fori_loop(0, phases, combine, 0)

        def density(n, _):
            at = pl.ds(pl.multiple_of(n * 256, 256), 256)
            acc[:, at] += jnp.dot(
                amp[...], whole[q, h, :, :, :, at].reshape(CAP * HALF, 256),
                preferred_element_type=jnp.float32,
            )
            return 0

        lax.fori_loop(0, acc.shape[1] // 256, density, 0)

    def step(t, _):
        pl.when(2 * t < phases)(lambda: begin(2 * t))
        pl.when(2 * t + 1 < phases)(lambda: begin(2 * t + 1))
        pl.when((t >= 1) & (t < phases + 1))(lambda: forward(t - 1))
        pl.when((t >= 2) & (t < phases + 2))(lambda: relay_far(t - 2))
        pl.when(t >= 3)(
            lambda: compute(t - 3, 1 - y, (B_ACROSS, B_LEFT_X, B_RIGHT_X, B_FAR_X))
        )

        @pl.when((t >= 2) & (t < phases + 2))
        def _():
            compute(t - 2, y, (B_OWN, B_LEFT, B_RIGHT, B_FAR))
            relay_rest(t - 2)

        return 0

    lax.fori_loop(0, phases + 3, step, 0)

    for q in range(phases):
        for i in range(CAP):
            row = (q * CAP + i) * ROWS
            out[i, q * ROWS:(q + 1) * ROWS, :] = acc[row:row + ROWS, :].astype(out.dtype)

    def drain(q, _):
        for d in range(1, N_OCC):
            exchange(q, d).wait_send()
        for kind in range(N_LINK):
            sends[kind](q).wait_send()
        for kind in range(N_SIB):
            share(q, kind).wait_send()
        return 0

    lax.fori_loop(0, phases, drain, 0)


def on_device(basis_integrals, group_sizes, orbital_order, eps_occ, eps_vir):
    window, vir_width, slab = basis_integrals.shape
    phases = vir_width // ROWS
    naux = slab * N_OCC
    rows = phases * CAP * ROWS
    eps_lanes = eps_vir.reshape(4, 2, 2, phases, ROWS).transpose(3, 1, 0, 2, 4)
    eps_lanes = eps_lanes.reshape(phases * 2, HALF)
    dma = pltpu.SemaphoreType.DMA
    vmem = pl.BlockSpec(memory_space=pltpu.VMEM)
    smem = pl.BlockSpec(memory_space=pltpu.SMEM)
    density = pl.pallas_call(
        functools.partial(kernel, phases),
        out_shape=jax.ShapeDtypeStruct((CAP, vir_width, naux), jnp.bfloat16),
        in_specs=[smem, smem, smem, vmem, vmem],
        out_specs=vmem,
        scratch_shapes=[
            pltpu.VMEM((phases, 2, CAP, N_VIRT // 2, ROWS, naux), jnp.bfloat16),
            pltpu.VMEM((rows, naux), jnp.bfloat16),
            pltpu.VMEM((CAP // 2, rows, 2 * HALF), jnp.float32),
            pltpu.VMEM((rows, CAP * HALF), jnp.bfloat16),
            pltpu.VMEM((rows, naux), jnp.float32),
            pltpu.VMEM((phases, N_OCC, CAP, ROWS, slab), jnp.bfloat16),
            pltpu.VMEM((rows, HALF), jnp.float32),
            pltpu.VMEM((phases, 2, CAP, HALF), jnp.float32),
            dma((phases, N_OCC - 1)),
            dma((phases, N_OCC - 1)),
            dma((phases, N_LINK)),
            dma((phases, N_LINK)),
            dma((phases, N_SIB)),
            dma((phases, N_SIB)),
            dma((phases,)),
        ],
        compiler_params=pltpu.CompilerParams(
            collective_id=0, has_side_effects=True, vmem_limit_bytes=60 * 1024 * 1024
        ),
    )(group_sizes, orbital_order, eps_occ, basis_integrals, eps_lanes)
    return density[None]


def solution(mesh):
    return jax.shard_map(
        on_device,
        mesh=mesh,
        in_specs=(P(None, "virt", "occ"), P(), P(), P(), P()),
        out_specs=P("occ", None, "virt", None),
        check_vma=False,
    )
```

```python
import functools

import jax
import jax.numpy as jnp
from jax import lax
from jax.experimental import pallas as pl
from jax.experimental.pallas import tpu as pltpu
from jax.sharding import PartitionSpec as P

CAP = 6
N_OCC = 8
N_VIRT = 16
ROWS = 16
HALF = 8 * ROWS
MESH = pl.DeviceIdType.MESH

LEFT, RIGHT, ACROSS, FAR_A, FAR_B, LEFT_X, RIGHT_X, FAR_X = range(8)
N_LINK = 8
B_OWN, B_LEFT, B_RIGHT, B_ACROSS, B_FAR, B_LEFT_X, B_RIGHT_X, B_FAR_X = range(8)
N_SIB = 8


def kernel(
    phases, sizes, order, eps_occ, basis, eps_vir, out,
    whole, own, coul, amp, acc, outgoing, row_gap, col_gap,
    a2a_send, a2a_recv, link_send, link_recv, sib_send, sib_recv, local_sem,
):
    occ = lax.axis_index("occ")
    me = lax.axis_index("virt")
    x, y, core = me // 4, (me // 2) % 2, me % 2
    slab = outgoing.shape[4]
    rows_per = CAP * ROWS

    def device(dx, flip):
        return (x + dx) % 4 * 4 + (y + flip) % 2 * 2 + core

    def place(dx, flip):
        return (y + flip) % 2, (x + dx) % 4 * 2 + core

    right, left, across = device(1, 0), device(3, 0), device(0, 1)
    sibling = me + 1 - 2 * core
    column_of = x * 2 + core
    mine = place(0, 0)

    barrier = pltpu.get_barrier_semaphore()
    for d in range(1, N_OCC):
        pl.semaphore_signal(
            barrier, inc=1, device_id={"occ": (occ + d) % N_OCC}, device_id_type=MESH
        )
    for peer in (right, left, across, sibling):
        pl.semaphore_signal(barrier, inc=1, device_id={"virt": peer}, device_id_type=MESH)

    offset = jnp.int32(0)
    energy = [jnp.float32(0.0)] * CAP
    for g in range(N_OCC):
        size = sizes[g]
        for s in range(CAP):
            orbital = order[jnp.minimum(offset + s, order.shape[0] - 1)]
            alive = jnp.where(s < size, 1.0, 0.0)
            block = basis[orbital] * jnp.full((phases * ROWS, slab), alive).astype(jnp.bfloat16)
            for q in range(phases):
                outgoing[q, g, s] = block[q * ROWS:(q + 1) * ROWS]
            energy[s] = jnp.where(occ == g, alive * eps_occ[orbital], energy[s])
        offset = offset + size
    pl.semaphore_wait(barrier, N_OCC + 3)

    my_slab = pl.ds(pl.multiple_of(occ * slab, slab), slab)

    def exchange(q, d):
        target = (occ + d) % N_OCC
        return pltpu.make_async_remote_copy(
            src_ref=outgoing.at[q, target],
            dst_ref=whole.at[q, y, :, column_of, :, my_slab],
            send_sem=a2a_send.at[q, d - 1],
            recv_sem=a2a_recv.at[q, d - 1],
            device_id={"occ": target},
            device_id_type=MESH,
        )

    def keep(q):
        return pltpu.make_async_copy(
            outgoing.at[q, occ], whole.at[q, y, :, column_of, :, my_slab], local_sem.at[q]
        )

    def link(q, source, kind, peer, first=0, count=CAP):
        part = whole.at[q, source[0], pl.ds(first, count), source[1]]
        return pltpu.make_async_remote_copy(
            src_ref=part, dst_ref=part,
            send_sem=link_send.at[q, kind], recv_sem=link_recv.at[q, kind],
            device_id={"virt": peer}, device_id_type=MESH,
        )

    half = CAP // 2
    sends = {
        LEFT: (lambda q: link(q, mine, LEFT, right)),
        RIGHT: (lambda q: link(q, mine, RIGHT, left)),
        ACROSS: (lambda q: link(q, mine, ACROSS, across)),
        FAR_A: (lambda q: link(q, place(3, 0), FAR_A, right, 0, half)),
        FAR_B: (lambda q: link(q, place(1, 0), FAR_B, left, half, CAP - half)),
        LEFT_X: (lambda q: link(q, place(0, 1), LEFT_X, right)),
        RIGHT_X: (lambda q: link(q, place(0, 1), RIGHT_X, left)),
        FAR_X: (lambda q: link(q, place(2, 0), FAR_X, across)),
    }
    held = {
        B_OWN: mine, B_LEFT: place(3, 0), B_RIGHT: place(1, 0), B_ACROSS: place(0, 1),
        B_FAR: place(2, 0), B_LEFT_X: place(3, 1), B_RIGHT_X: place(1, 1), B_FAR_X: place(2, 1),
    }

    def share(q, kind):
        part = whole.at[q, held[kind][0], :, held[kind][1]]
        return pltpu.make_async_remote_copy(
            src_ref=part, dst_ref=part,
            send_sem=sib_send.at[q, kind], recv_sem=sib_recv.at[q, kind],
            device_id={"virt": sibling}, device_id_type=MESH,
        )

    def launch(q, _):
        for d in range(1, N_OCC):
            exchange(q, d).start()
        keep(q).start()
        return 0

    lax.fori_loop(0, phases, launch, 0)

    lane = lax.broadcasted_iota(jnp.int32, (ROWS, HALF), 1)
    sub = lax.broadcasted_iota(jnp.int32, (ROWS, HALF), 0)
    first_lane = column_of * ROWS
    for q in range(phases):
        spread = jnp.broadcast_to(eps_vir[pl.ds(q * 2 + y, 1), :], (ROWS, HALF))
        column = jnp.sum(
            jnp.where(lane == sub + first_lane, spread, 0.0), axis=1, keepdims=True
        )
        for i in range(CAP):
            at = (q * CAP + i) * ROWS
            row_gap[at:at + ROWS, :] = energy[i] - jnp.broadcast_to(column, (ROWS, HALF))
            for h in range(2):
                col_gap[q, h, i:i + 1, :] = energy[i] - eps_vir[q * 2 + h:q * 2 + h + 1, :]
    acc[...] = jnp.zeros_like(acc)

    def gather_rows(q):
        for d in range(1, N_OCC):
            exchange(q, d).wait_recv()
        keep(q).wait()
        own[pl.ds(pl.multiple_of(q * rows_per, rows_per), rows_per), :] = whole[
            q, y, :, column_of
        ].reshape(rows_per, own.shape[1])

    def send_own(q):
        for kind in (LEFT, RIGHT, ACROSS):
            sends[kind](q).start()
        share(q, B_OWN).start()

    def forward_far(q):
        sends[LEFT](q).wait_recv()
        sends[FAR_A](q).start()
        share(q, B_LEFT).start()
        sends[RIGHT](q).wait_recv()
        sends[FAR_B](q).start()
        share(q, B_RIGHT).start()

    def forward_across(q):
        sends[ACROSS](q).wait_recv()
        sends[LEFT_X](q).start()
        sends[RIGHT_X](q).start()
        share(q, B_ACROSS).start()

    def relay_far(q):
        sends[FAR_A](q).wait_recv()
        sends[FAR_B](q).wait_recv()
        sends[FAR_X](q).start()
        share(q, B_FAR).start()

    def relay_rest(q):
        sends[LEFT_X](q).wait_recv()
        share(q, B_LEFT_X).start()
        sends[RIGHT_X](q).wait_recv()
        share(q, B_RIGHT_X).start()
        sends[FAR_X](q).wait_recv()
        share(q, B_FAR_X).start()

    def compute(q, h, kinds):
        for kind in kinds:
            share(q, kind).wait_recv()

        def coulomb(j, _):
            coul[j] = lax.dot_general(
                own[...], whole[q, h, pl.ds(j * 2, 2)].reshape(2 * HALF, own.shape[1]),
                (((1,), (1,)), ((), ())), preferred_element_type=jnp.float32,
            )
            return 0

        lax.fori_loop(0, CAP // 2, coulomb, 0, unroll=True)

        def combine(p, _):
            def lanes(j):
                return slice(j % 2 * HALF, (j % 2 + 1) * HALF)

            for i in range(CAP):
                at_i = pl.ds(pl.multiple_of(p * rows_per + i * ROWS, ROWS), ROWS)
                gap_i = row_gap[at_i, :]
                for j in range(i, CAP):
                    at_j = pl.ds(pl.multiple_of(p * rows_per + j * ROWS, ROWS), ROWS)
                    inverse = 1.0 / (gap_i + col_gap[q, h, pl.ds(j, 1), :])
                    direct = coul[j // 2, at_i, lanes(j)]
                    swapped = coul[i // 2, at_j, lanes(i)]
                    amp[at_i, j * HALF:(j + 1) * HALF] = (
                        (2.0 * direct - swapped) * inverse
                    ).astype(jnp.bfloat16)
                    if i != j:
                        amp[at_j, i * HALF:(i + 1) * HALF] = (
                            (2.0 * swapped - direct) * inverse
                        ).astype(jnp.bfloat16)
            return 0

        lax.fori_loop(0, phases, combine, 0)

        def density(n, _):
            at = pl.ds(pl.multiple_of(n * 512, 512), 512)
            acc[:, at] += jnp.dot(
                amp[...], whole[q, h, :, :, :, at].reshape(CAP * HALF, 512),
                preferred_element_type=jnp.float32,
            )
            return 0

        lax.fori_loop(0, acc.shape[1] // 512, density, 0, unroll=True)

    final = phases - 1
    for q in range(phases):
        gather_rows(q)
        if q < max(final, 1):
            send_own(q)
        if 1 <= q <= 2:
            forward_far(q - 1)
        if q == 2:
            forward_across(0)

    def step(k, _):
        @pl.when(k < phases)
        def _():
            relay_far(k)
            compute(k, y, (B_OWN, B_LEFT, B_RIGHT, B_FAR))

        @pl.when(k >= 1)
        def _():
            relay_rest(k - 1)
            compute(k - 1, 1 - y, (B_ACROSS, B_LEFT_X, B_RIGHT_X, B_FAR_X))

        pl.when(k == 0)(lambda: send_own(final))
        pl.when(k + 2 < phases)(lambda: forward_far(k + 2))
        pl.when(k + 2 < phases)(lambda: forward_across(k + 1))
        pl.when(k + 3 == phases)(lambda: forward_across(final))
        return 0

    lax.fori_loop(0, phases + 1, step, 0)

    for q in range(phases):
        for i in range(CAP):
            row = (q * CAP + i) * ROWS
            out[i, q * ROWS:(q + 1) * ROWS, :] = acc[row:row + ROWS, :].astype(out.dtype)

    def drain(q, _):
        for d in range(1, N_OCC):
            exchange(q, d).wait_send()
        for kind in range(N_LINK):
            sends[kind](q).wait_send()
        for kind in range(N_SIB):
            share(q, kind).wait_send()
        return 0

    lax.fori_loop(0, phases, drain, 0)


def on_device(basis_integrals, group_sizes, orbital_order, eps_occ, eps_vir):
    window, vir_width, slab = basis_integrals.shape
    phases = vir_width // ROWS
    naux = slab * N_OCC
    rows = phases * CAP * ROWS
    eps_lanes = eps_vir.reshape(4, 2, 2, phases, ROWS).transpose(3, 1, 0, 2, 4)
    eps_lanes = eps_lanes.reshape(phases * 2, HALF)
    dma = pltpu.SemaphoreType.DMA
    vmem = pl.BlockSpec(memory_space=pltpu.VMEM)
    smem = pl.BlockSpec(memory_space=pltpu.SMEM)
    density = pl.pallas_call(
        functools.partial(kernel, phases),
        out_shape=jax.ShapeDtypeStruct((CAP, vir_width, naux), jnp.bfloat16),
        in_specs=[smem, smem, smem, vmem, vmem],
        out_specs=vmem,
        scratch_shapes=[
            pltpu.VMEM((phases, 2, CAP, N_VIRT // 2, ROWS, naux), jnp.bfloat16),
            pltpu.VMEM((rows, naux), jnp.bfloat16),
            pltpu.VMEM((CAP // 2, rows, 2 * HALF), jnp.float32),
            pltpu.VMEM((rows, CAP * HALF), jnp.bfloat16),
            pltpu.VMEM((rows, naux), jnp.float32),
            pltpu.VMEM((phases, N_OCC, CAP, ROWS, slab), jnp.bfloat16),
            pltpu.VMEM((rows, HALF), jnp.float32),
            pltpu.VMEM((phases, 2, CAP, HALF), jnp.float32),
            dma((phases, N_OCC - 1)),
            dma((phases, N_OCC - 1)),
            dma((phases, N_LINK)),
            dma((phases, N_LINK)),
            dma((phases, N_SIB)),
            dma((phases, N_SIB)),
            dma((phases,)),
        ],
        compiler_params=pltpu.CompilerParams(
            collective_id=0, has_side_effects=True, vmem_limit_bytes=47 * 1024 * 1024
        ),
    )(group_sizes, orbital_order, eps_occ, basis_integrals, eps_lanes)
    return density[None]


def solution(mesh):
    return jax.shard_map(
        on_device,
        mesh=mesh,
        in_specs=(P(None, "virt", "occ"), P(), P(), P(), P()),
        out_specs=P("occ", None, "virt", None),
        check_vma=False,
    )
```

```python
import functools

import jax
import jax.numpy as jnp
from jax import lax
from jax.experimental import pallas as pl
from jax.experimental.pallas import tpu as pltpu
from jax.sharding import PartitionSpec as P

CAP = 6
N_OCC = 8
N_VIRT = 16
ROWS = 16
HALF = 8 * ROWS
MESH = pl.DeviceIdType.MESH

LEFT, RIGHT, ACROSS, FAR_A, FAR_B, LEFT_X, RIGHT_X, FAR_X = range(8)
N_LINK = 8
B_OWN, B_LEFT, B_RIGHT, B_ACROSS, B_FAR, B_LEFT_X, B_RIGHT_X, B_FAR_X = range(8)
N_SIB = 8


def kernel(
    phases, sizes, order, eps_occ, basis_hbm, eps_vir, out,
    whole, own, coul, amp, acc, outgoing, row_gap, col_gap,
    eps_half, basis, basis_sem, a2a_send, a2a_recv, link_send, link_recv, sib_send, sib_recv, local_sem,
):
    occ = lax.axis_index("occ")
    me = lax.axis_index("virt")
    x, y, core = me // 4, (me // 2) % 2, me % 2
    slab = outgoing.shape[4]
    rows_per = CAP * ROWS

    def device(dx, flip):
        return (x + dx) % 4 * 4 + (y + flip) % 2 * 2 + core

    def place(dx, flip):
        return (y + flip) % 2, (x + dx) % 4 * 2 + core

    right, left, across = device(1, 0), device(3, 0), device(0, 1)
    sibling = me + 1 - 2 * core
    column_of = x * 2 + core
    mine = place(0, 0)

    fetch = pltpu.make_async_copy(basis_hbm, basis, basis_sem)
    fetch.start()
    barrier = pltpu.get_barrier_semaphore()
    for d in range(1, N_OCC):
        pl.semaphore_signal(
            barrier, inc=1, device_id={"occ": (occ + d) % N_OCC}, device_id_type=MESH
        )
    for peer in (right, left, across, sibling):
        pl.semaphore_signal(barrier, inc=1, device_id={"virt": peer}, device_id_type=MESH)

    fetch.wait()
    offset = jnp.int32(0)
    energy = [jnp.float32(0.0)] * CAP
    for g in range(N_OCC):
        size = sizes[g]
        for s in range(CAP):
            orbital = order[jnp.minimum(offset + s, order.shape[0] - 1)]
            alive = jnp.where(s < size, 1.0, 0.0)
            block = basis[orbital] * jnp.full((phases * ROWS, slab), alive).astype(jnp.bfloat16)
            for q in range(phases):
                outgoing[q, g, s] = block[q * ROWS:(q + 1) * ROWS]
            energy[s] = jnp.where(occ == g, alive * eps_occ[orbital], energy[s])
        offset = offset + size
    pl.semaphore_wait(barrier, N_OCC + 3)

    my_slab = pl.ds(pl.multiple_of(occ * slab, slab), slab)

    def exchange(q, d):
        target = (occ + d) % N_OCC
        return pltpu.make_async_remote_copy(
            src_ref=outgoing.at[q, target],
            dst_ref=whole.at[q, y, :, column_of, :, my_slab],
            send_sem=a2a_send.at[q, d - 1],
            recv_sem=a2a_recv.at[q, d - 1],
            device_id={"occ": target},
            device_id_type=MESH,
        )

    def keep(q):
        return pltpu.make_async_copy(
            outgoing.at[q, occ], whole.at[q, y, :, column_of, :, my_slab], local_sem.at[q]
        )

    def link(q, source, kind, peer, first=0, count=CAP):
        part = whole.at[q, source[0], pl.ds(first, count), source[1]]
        return pltpu.make_async_remote_copy(
            src_ref=part, dst_ref=part,
            send_sem=link_send.at[q, kind], recv_sem=link_recv.at[q, kind],
            device_id={"virt": peer}, device_id_type=MESH,
        )

    half = CAP // 2
    sends = {
        LEFT: (lambda q: link(q, mine, LEFT, right)),
        RIGHT: (lambda q: link(q, mine, RIGHT, left)),
        ACROSS: (lambda q: link(q, mine, ACROSS, across)),
        FAR_A: (lambda q: link(q, place(3, 0), FAR_A, right, 0, half)),
        FAR_B: (lambda q: link(q, place(1, 0), FAR_B, left, half, CAP - half)),
        LEFT_X: (lambda q: link(q, place(0, 1), LEFT_X, right)),
        RIGHT_X: (lambda q: link(q, place(0, 1), RIGHT_X, left)),
        FAR_X: (lambda q: link(q, place(2, 0), FAR_X, across)),
    }
    held = {
        B_OWN: mine, B_LEFT: place(3, 0), B_RIGHT: place(1, 0), B_ACROSS: place(0, 1),
        B_FAR: place(2, 0), B_LEFT_X: place(3, 1), B_RIGHT_X: place(1, 1), B_FAR_X: place(2, 1),
    }

    def share(q, kind):
        part = whole.at[q, held[kind][0], :, held[kind][1]]
        return pltpu.make_async_remote_copy(
            src_ref=part, dst_ref=part,
            send_sem=sib_send.at[q, kind], recv_sem=sib_recv.at[q, kind],
            device_id={"virt": sibling}, device_id_type=MESH,
        )

    def launch(q, _):
        for d in range(1, N_OCC):
            exchange(q, d).start()
        keep(q).start()
        return 0

    lax.fori_loop(0, phases, launch, 0)

    lane = lax.broadcasted_iota(jnp.int32, (ROWS, HALF), 1)
    sub = lax.broadcasted_iota(jnp.int32, (ROWS, HALF), 0)
    first_lane = column_of * ROWS
    for q in range(phases):
        for h in range(2):
            lanes = jnp.zeros((1, HALF), jnp.float32)
            for k in range(8):
                chunk = (k // 2 * 4 + h * 2 + k % 2) * phases + q
                piece = eps_vir[chunk // 8:chunk // 8 + 1, :]
                shift = (k - chunk % 8) % 8 * ROWS
                piece = pltpu.roll(piece, shift, 1) if shift else piece
                lanes = jnp.where(lane[:1] // ROWS == k, piece, lanes)
            eps_half[q, h:h + 1, :] = lanes
    for q in range(phases):
        spread = jnp.broadcast_to(eps_half[q, pl.ds(y, 1), :], (ROWS, HALF))
        column = jnp.sum(
            jnp.where(lane == sub + first_lane, spread, 0.0), axis=1, keepdims=True
        )
        for i in range(CAP):
            at = (q * CAP + i) * ROWS
            row_gap[at:at + ROWS, :] = energy[i] - jnp.broadcast_to(column, (ROWS, HALF))
            for h in range(2):
                col_gap[q, h, i:i + 1, :] = energy[i] - eps_half[q, h:h + 1, :]
    acc[...] = jnp.zeros_like(acc)

    def gather_rows(q):
        for d in range(1, N_OCC):
            exchange(q, d).wait_recv()
        keep(q).wait()
        own[pl.ds(pl.multiple_of(q * rows_per, rows_per), rows_per), :] = whole[
            q, y, :, column_of
        ].reshape(rows_per, own.shape[1])

    def send_own(q):
        for kind in (LEFT, RIGHT, ACROSS):
            sends[kind](q).start()
        share(q, B_OWN).start()

    def forward_far(q):
        sends[LEFT](q).wait_recv()
        sends[FAR_A](q).start()
        share(q, B_LEFT).start()
        sends[RIGHT](q).wait_recv()
        sends[FAR_B](q).start()
        share(q, B_RIGHT).start()

    def forward_across(q):
        sends[ACROSS](q).wait_recv()
        sends[LEFT_X](q).start()
        sends[RIGHT_X](q).start()
        share(q, B_ACROSS).start()

    def relay_far(q):
        sends[FAR_A](q).wait_recv()
        sends[FAR_B](q).wait_recv()
        sends[FAR_X](q).start()
        share(q, B_FAR).start()

    def relay_rest(q):
        sends[LEFT_X](q).wait_recv()
        share(q, B_LEFT_X).start()
        sends[RIGHT_X](q).wait_recv()
        share(q, B_RIGHT_X).start()
        sends[FAR_X](q).wait_recv()
        share(q, B_FAR_X).start()

    def compute(q, h, kinds):
        for kind in kinds:
            share(q, kind).wait_recv()

        def coulomb(j, _):
            coul[j] = lax.dot_general(
                own[...], whole[q, h, pl.ds(j * 2, 2)].reshape(2 * HALF, own.shape[1]),
                (((1,), (1,)), ((), ())), preferred_element_type=jnp.float32,
            )
            return 0

        lax.fori_loop(0, CAP // 2, coulomb, 0, unroll=True)

        def combine(p, _):
            def lanes(j):
                return slice(j % 2 * HALF, (j % 2 + 1) * HALF)

            for i in range(CAP):
                at_i = pl.ds(pl.multiple_of(p * rows_per + i * ROWS, ROWS), ROWS)
                gap_i = row_gap[at_i, :]
                for j in range(i, CAP):
                    at_j = pl.ds(pl.multiple_of(p * rows_per + j * ROWS, ROWS), ROWS)
                    inverse = 1.0 / (gap_i + col_gap[q, h, pl.ds(j, 1), :])
                    direct = coul[j // 2, at_i, lanes(j)]
                    swapped = coul[i // 2, at_j, lanes(i)]
                    amp[at_i, j * HALF:(j + 1) * HALF] = (
                        (2.0 * direct - swapped) * inverse
                    ).astype(jnp.bfloat16)
                    if i != j:
                        amp[at_j, i * HALF:(i + 1) * HALF] = (
                            (2.0 * swapped - direct) * inverse
                        ).astype(jnp.bfloat16)
            return 0

        lax.fori_loop(0, phases, combine, 0)

        def density(n, _):
            at = pl.ds(pl.multiple_of(n * 512, 512), 512)
            acc[:, at] += jnp.dot(
                amp[...], whole[q, h, :, :, :, at].reshape(CAP * HALF, 512),
                preferred_element_type=jnp.float32,
            )
            return 0

        lax.fori_loop(0, acc.shape[1] // 512, density, 0, unroll=True)

    final = phases - 1
    for q in range(phases):
        gather_rows(q)
        if q < max(final, 1):
            send_own(q)
        if 1 <= q <= 2:
            forward_far(q - 1)
        if q == 2:
            forward_across(0)

    def step(k, _):
        @pl.when(k < phases)
        def _():
            relay_far(k)
            compute(k, y, (B_OWN, B_LEFT, B_RIGHT, B_FAR))

        pl.when(k == 0)(lambda: send_own(final))
        pl.when(k + 2 < phases)(lambda: forward_far(k + 2))
        pl.when(k + 2 < phases)(lambda: forward_across(k + 1))
        pl.when(k + 3 == phases)(lambda: forward_across(final))

        @pl.when(k >= 1)
        def _():
            relay_rest(k - 1)
            compute(k - 1, 1 - y, (B_ACROSS, B_LEFT_X, B_RIGHT_X, B_FAR_X))

        return 0

    lax.fori_loop(0, phases + 1, step, 0)

    for q in range(phases):
        for i in range(CAP):
            row = (q * CAP + i) * ROWS
            out[i, q * ROWS:(q + 1) * ROWS, :] = acc[row:row + ROWS, :].astype(out.dtype)

    def drain(q, _):
        for d in range(1, N_OCC):
            exchange(q, d).wait_send()
        for kind in range(N_LINK):
            sends[kind](q).wait_send()
        for kind in range(N_SIB):
            share(q, kind).wait_send()
        return 0

    lax.fori_loop(0, phases, drain, 0)


def on_device(basis_integrals, group_sizes, orbital_order, eps_occ, eps_vir):
    window, vir_width, slab = basis_integrals.shape
    phases = vir_width // ROWS
    naux = slab * N_OCC
    rows = phases * CAP * ROWS
    dma = pltpu.SemaphoreType.DMA
    vmem = pl.BlockSpec(memory_space=pltpu.VMEM)
    smem = pl.BlockSpec(memory_space=pltpu.SMEM)
    density = pl.pallas_call(
        functools.partial(kernel, phases),
        out_shape=jax.ShapeDtypeStruct((CAP, vir_width, naux), jnp.bfloat16),
        in_specs=[smem, smem, smem, pl.BlockSpec(memory_space=pltpu.HBM), vmem],
        out_specs=vmem,
        scratch_shapes=[
            pltpu.VMEM((phases, 2, CAP, N_VIRT // 2, ROWS, naux), jnp.bfloat16),
            pltpu.VMEM((rows, naux), jnp.bfloat16),
            pltpu.VMEM((CAP // 2, rows, 2 * HALF), jnp.float32),
            pltpu.VMEM((rows, CAP * HALF), jnp.bfloat16),
            pltpu.VMEM((rows, naux), jnp.float32),
            pltpu.VMEM((phases, N_OCC, CAP, ROWS, slab), jnp.bfloat16),
            pltpu.VMEM((rows, HALF), jnp.float32),
            pltpu.VMEM((phases, 2, CAP, HALF), jnp.float32),
            pltpu.VMEM((phases, 2, HALF), jnp.float32),
            pltpu.VMEM((window, vir_width, slab), jnp.bfloat16),
            dma,
            dma((phases, N_OCC - 1)),
            dma((phases, N_OCC - 1)),
            dma((phases, N_LINK)),
            dma((phases, N_LINK)),
            dma((phases, N_SIB)),
            dma((phases, N_SIB)),
            dma((phases,)),
        ],
        compiler_params=pltpu.CompilerParams(
            collective_id=0, has_side_effects=True, vmem_limit_bytes=60 * 1024 * 1024
        ),
    )(group_sizes, orbital_order, eps_occ, basis_integrals, eps_vir.reshape(-1, HALF))
    return density[None]


def solution(mesh):
    return jax.shard_map(
        on_device,
        mesh=mesh,
        in_specs=(P(None, "virt", "occ"), P(), P(), P(), P()),
        out_specs=P("occ", None, "virt", None),
        check_vma=False,
    )
```

```python
import functools

import jax
import jax.numpy as jnp
from jax import lax
from jax.experimental import pallas as pl
from jax.experimental.pallas import tpu as pltpu
from jax.sharding import PartitionSpec as P

CAP = 6
N_OCC = 8
N_VIRT = 16
ROWS = 16
HALF = 8 * ROWS
MESH = pl.DeviceIdType.MESH

LEFT, RIGHT, ACROSS, FAR_A, FAR_B, LEFT_X, RIGHT_X, FAR_X = range(8)
N_LINK = 8
B_OWN, B_LEFT, B_RIGHT, B_ACROSS, B_FAR, B_LEFT_X, B_RIGHT_X, B_FAR_X = range(8)
N_SIB = 8


def kernel(
    phases, sizes, order, eps_occ, basis_hbm, eps_vir, out,
    whole, own, coul, amp, acc, outgoing, row_gap, col_gap,
    eps_half, basis, basis_sem, a2a_send, a2a_recv, link_send, link_recv, sib_send, sib_recv, local_sem,
):
    occ = lax.axis_index("occ")
    me = lax.axis_index("virt")
    x, y, core = me // 4, (me // 2) % 2, me % 2
    slab = outgoing.shape[4]
    rows_per = CAP * ROWS

    def device(dx, flip):
        return (x + dx) % 4 * 4 + (y + flip) % 2 * 2 + core

    def place(dx, flip):
        return (y + flip) % 2, (x + dx) % 4 * 2 + core

    right, left, across = device(1, 0), device(3, 0), device(0, 1)
    sibling = me + 1 - 2 * core
    column_of = x * 2 + core
    mine = place(0, 0)

    fetch = pltpu.make_async_copy(basis_hbm, basis, basis_sem)
    fetch.start()
    barrier = pltpu.get_barrier_semaphore()
    for d in range(1, N_OCC):
        pl.semaphore_signal(
            barrier, inc=1, device_id={"occ": (occ + d) % N_OCC}, device_id_type=MESH
        )
    for peer in (right, left, across, sibling):
        pl.semaphore_signal(barrier, inc=1, device_id={"virt": peer}, device_id_type=MESH)

    fetch.wait()
    offset = jnp.int32(0)
    energy = [jnp.float32(0.0)] * CAP
    for g in range(N_OCC):
        size = sizes[g]
        for s in range(CAP):
            orbital = order[jnp.minimum(offset + s, order.shape[0] - 1)]
            alive = jnp.where(s < size, 1.0, 0.0)
            block = basis[orbital] * jnp.full((phases * ROWS, slab), alive).astype(jnp.bfloat16)
            for q in range(phases):
                outgoing[q, g, s] = block[q * ROWS:(q + 1) * ROWS]
            energy[s] = jnp.where(occ == g, alive * eps_occ[orbital], energy[s])
        offset = offset + size
    pl.semaphore_wait(barrier, N_OCC + 3)

    my_slab = pl.ds(pl.multiple_of(occ * slab, slab), slab)

    def exchange(q, d):
        target = (occ + d) % N_OCC
        return pltpu.make_async_remote_copy(
            src_ref=outgoing.at[q, target],
            dst_ref=whole.at[q, y, :, column_of, :, my_slab],
            send_sem=a2a_send.at[q, d - 1],
            recv_sem=a2a_recv.at[q, d - 1],
            device_id={"occ": target},
            device_id_type=MESH,
        )

    def keep(q):
        return pltpu.make_async_copy(
            outgoing.at[q, occ], whole.at[q, y, :, column_of, :, my_slab], local_sem.at[q]
        )

    def link(q, source, kind, peer, first=0, count=CAP):
        part = whole.at[q, source[0], pl.ds(first, count), source[1]]
        return pltpu.make_async_remote_copy(
            src_ref=part, dst_ref=part,
            send_sem=link_send.at[q, kind], recv_sem=link_recv.at[q, kind],
            device_id={"virt": peer}, device_id_type=MESH,
        )

    half = CAP // 2
    sends = {
        LEFT: (lambda q: link(q, mine, LEFT, right)),
        RIGHT: (lambda q: link(q, mine, RIGHT, left)),
        ACROSS: (lambda q: link(q, mine, ACROSS, across)),
        FAR_A: (lambda q: link(q, place(3, 0), FAR_A, right, 0, half)),
        FAR_B: (lambda q: link(q, place(1, 0), FAR_B, left, half, CAP - half)),
        LEFT_X: (lambda q: link(q, place(0, 1), LEFT_X, right)),
        RIGHT_X: (lambda q: link(q, place(0, 1), RIGHT_X, left)),
        FAR_X: (lambda q: link(q, place(2, 0), FAR_X, across)),
    }
    held = {
        B_OWN: mine, B_LEFT: place(3, 0), B_RIGHT: place(1, 0), B_ACROSS: place(0, 1),
        B_FAR: place(2, 0), B_LEFT_X: place(3, 1), B_RIGHT_X: place(1, 1), B_FAR_X: place(2, 1),
    }

    def share(q, kind):
        part = whole.at[q, held[kind][0], :, held[kind][1]]
        return pltpu.make_async_remote_copy(
            src_ref=part, dst_ref=part,
            send_sem=sib_send.at[q, kind], recv_sem=sib_recv.at[q, kind],
            device_id={"virt": sibling}, device_id_type=MESH,
        )

    def launch(q):
        for d in range(1, N_OCC):
            exchange(q, d).start()
        keep(q).start()
        return 0

    launch(0)

    lane = lax.broadcasted_iota(jnp.int32, (ROWS, HALF), 1)
    sub = lax.broadcasted_iota(jnp.int32, (ROWS, HALF), 0)
    first_lane = column_of * ROWS
    for q in range(phases):
        for h in range(2):
            lanes = jnp.zeros((1, HALF), jnp.float32)
            for k in range(8):
                chunk = (k // 2 * 4 + h * 2 + k % 2) * phases + q
                piece = eps_vir[chunk // 8:chunk // 8 + 1, :]
                shift = (k - chunk % 8) % 8 * ROWS
                piece = pltpu.roll(piece, shift, 1) if shift else piece
                lanes = jnp.where(lane[:1] // ROWS == k, piece, lanes)
            eps_half[q, h:h + 1, :] = lanes
    for q in range(phases):
        spread = jnp.broadcast_to(eps_half[q, pl.ds(y, 1), :], (ROWS, HALF))
        column = jnp.sum(
            jnp.where(lane == sub + first_lane, spread, 0.0), axis=1, keepdims=True
        )
        for i in range(CAP):
            at = (q * CAP + i) * ROWS
            row_gap[at:at + ROWS, :] = energy[i] - jnp.broadcast_to(column, (ROWS, HALF))
            for h in range(2):
                col_gap[q, h, i:i + 1, :] = energy[i] - eps_half[q, h:h + 1, :]
    acc[...] = jnp.zeros_like(acc)

    def gather_rows(q):
        for d in range(1, N_OCC):
            exchange(q, d).wait_recv()
        keep(q).wait()
        if q + 1 < phases:
            launch(q + 1)
        own[pl.ds(pl.multiple_of(q * rows_per, rows_per), rows_per), :] = whole[
            q, y, :, column_of
        ].reshape(rows_per, own.shape[1])

    def send_own(q):
        for kind in (LEFT, RIGHT, ACROSS):
            sends[kind](q).start()
        share(q, B_OWN).start()

    def forward_far(q):
        sends[LEFT](q).wait_recv()
        sends[FAR_A](q).start()
        share(q, B_LEFT).start()
        sends[RIGHT](q).wait_recv()
        sends[FAR_B](q).start()
        share(q, B_RIGHT).start()

    def forward_across(q):
        sends[ACROSS](q).wait_recv()
        sends[LEFT_X](q).start()
        sends[RIGHT_X](q).start()
        share(q, B_ACROSS).start()

    def relay_far(q):
        sends[FAR_A](q).wait_recv()
        sends[FAR_B](q).wait_recv()
        sends[FAR_X](q).start()
        share(q, B_FAR).start()

    def relay_rest(q):
        sends[LEFT_X](q).wait_recv()
        share(q, B_LEFT_X).start()
        sends[RIGHT_X](q).wait_recv()
        share(q, B_RIGHT_X).start()
        sends[FAR_X](q).wait_recv()
        share(q, B_FAR_X).start()

    def compute(q, h, kinds):
        for kind in kinds:
            share(q, kind).wait_recv()

        def coulomb(j, _):
            coul[j] = lax.dot_general(
                own[...], whole[q, h, pl.ds(j * 2, 2)].reshape(2 * HALF, own.shape[1]),
                (((1,), (1,)), ((), ())), preferred_element_type=jnp.float32,
            )
            return 0

        lax.fori_loop(0, CAP // 2, coulomb, 0, unroll=True)

        def combine(p, _):
            def lanes(j):
                return slice(j % 2 * HALF, (j % 2 + 1) * HALF)

            for i in range(CAP):
                at_i = pl.ds(pl.multiple_of(p * rows_per + i * ROWS, ROWS), ROWS)
                gap_i = row_gap[at_i, :]
                for j in range(i, CAP):
                    at_j = pl.ds(pl.multiple_of(p * rows_per + j * ROWS, ROWS), ROWS)
                    inverse = 1.0 / (gap_i + col_gap[q, h, pl.ds(j, 1), :])
                    direct = coul[j // 2, at_i, lanes(j)]
                    swapped = coul[i // 2, at_j, lanes(i)]
                    amp[at_i, j * HALF:(j + 1) * HALF] = (
                        (2.0 * direct - swapped) * inverse
                    ).astype(jnp.bfloat16)
                    if i != j:
                        amp[at_j, i * HALF:(i + 1) * HALF] = (
                            (2.0 * swapped - direct) * inverse
                        ).astype(jnp.bfloat16)
            return 0

        lax.fori_loop(0, phases, combine, 0)

        def density(n, _):
            at = pl.ds(pl.multiple_of(n * 512, 512), 512)
            acc[:, at] += jnp.dot(
                amp[...], whole[q, h, :, :, :, at].reshape(CAP * HALF, 512),
                preferred_element_type=jnp.float32,
            )
            return 0

        lax.fori_loop(0, acc.shape[1] // 512, density, 0, unroll=True)

    final = phases - 1
    for q in range(phases):
        gather_rows(q)
        if q < max(final, 1):
            send_own(q)
        if 1 <= q <= 2:
            forward_far(q - 1)
        if q == 2:
            forward_across(0)

    def step(k, _):
        @pl.when(k < phases)
        def _():
            relay_far(k)
            compute(k, y, (B_OWN, B_LEFT, B_RIGHT, B_FAR))

        pl.when(k == 0)(lambda: send_own(final))
        pl.when(k + 2 < phases)(lambda: forward_far(k + 2))
        pl.when(k + 2 < phases)(lambda: forward_across(k + 1))
        pl.when(k + 3 == phases)(lambda: forward_across(final))

        @pl.when(k >= 1)
        def _():
            relay_rest(k - 1)
            compute(k - 1, 1 - y, (B_ACROSS, B_LEFT_X, B_RIGHT_X, B_FAR_X))

        return 0

    lax.fori_loop(0, phases + 1, step, 0)

    for q in range(phases):
        for i in range(CAP):
            row = (q * CAP + i) * ROWS
            out[i, q * ROWS:(q + 1) * ROWS, :] = acc[row:row + ROWS, :].astype(out.dtype)

    def drain(q, _):
        for d in range(1, N_OCC):
            exchange(q, d).wait_send()
        for kind in range(N_LINK):
            sends[kind](q).wait_send()
        for kind in range(N_SIB):
            share(q, kind).wait_send()
        return 0

    lax.fori_loop(0, phases, drain, 0)


def on_device(basis_integrals, group_sizes, orbital_order, eps_occ, eps_vir):
    window, vir_width, slab = basis_integrals.shape
    phases = vir_width // ROWS
    naux = slab * N_OCC
    rows = phases * CAP * ROWS
    dma = pltpu.SemaphoreType.DMA
    vmem = pl.BlockSpec(memory_space=pltpu.VMEM)
    smem = pl.BlockSpec(memory_space=pltpu.SMEM)
    density = pl.pallas_call(
        functools.partial(kernel, phases),
        out_shape=jax.ShapeDtypeStruct((CAP, vir_width, naux), jnp.bfloat16),
        in_specs=[smem, smem, smem, pl.BlockSpec(memory_space=pltpu.HBM), vmem],
        out_specs=vmem,
        scratch_shapes=[
            pltpu.VMEM((phases, 2, CAP, N_VIRT // 2, ROWS, naux), jnp.bfloat16),
            pltpu.VMEM((rows, naux), jnp.bfloat16),
            pltpu.VMEM((CAP // 2, rows, 2 * HALF), jnp.float32),
            pltpu.VMEM((rows, CAP * HALF), jnp.bfloat16),
            pltpu.VMEM((rows, naux), jnp.float32),
            pltpu.VMEM((phases, N_OCC, CAP, ROWS, slab), jnp.bfloat16),
            pltpu.VMEM((rows, HALF), jnp.float32),
            pltpu.VMEM((phases, 2, CAP, HALF), jnp.float32),
            pltpu.VMEM((phases, 2, HALF), jnp.float32),
            pltpu.VMEM((window, vir_width, slab), jnp.bfloat16),
            dma,
            dma((phases, N_OCC - 1)),
            dma((phases, N_OCC - 1)),
            dma((phases, N_LINK)),
            dma((phases, N_LINK)),
            dma((phases, N_SIB)),
            dma((phases, N_SIB)),
            dma((phases,)),
        ],
        compiler_params=pltpu.CompilerParams(
            collective_id=0, has_side_effects=True, vmem_limit_bytes=60 * 1024 * 1024
        ),
    )(group_sizes, orbital_order, eps_occ, basis_integrals, eps_vir.reshape(-1, HALF))
    return density[None]


def solution(mesh):
    return jax.shard_map(
        on_device,
        mesh=mesh,
        in_specs=(P(None, "virt", "occ"), P(), P(), P(), P()),
        out_specs=P("occ", None, "virt", None),
        check_vma=False,
    )
```
